32 devices in a mesh: rep: 8 (over y, x, core), shard: 4 (over z).
Axes of the slice: x: 2, y: 2, z: 4, core: 2. Of those that a mesh axis runs over, the one named last changes fastest.
Arguments:
- layer_input: bfloat16 [16384, 768], P(('rep', 'shard')), may hold values from -6 to 6
- query_weight: bfloat16 [768, 768], P('shard'), may hold values from -0.21875 to 0.21875
- key_weight: bfloat16 [768, 768], P('shard'), may hold values from -0.21875 to 0.21875
- value_weight: bfloat16 [768, 768], P('shard'), may hold values from -0.21875 to 0.21875
- output_weight: bfloat16 [768, 768], P('shard'), may hold values from -6 to 6
- inner_weight: bfloat16 [768, 3072], P('shard'), may hold values from -0.21875 to 0.21875
- outer_weight: bfloat16 [3072, 768], P('shard'), may hold values from -0.109375 to 0.109375
- query_bias: float32 [768], replicated, may hold values from -3 to 3
- value_bias: float32 [768], replicated, may hold values from -3 to 3
- output_bias: float32 [768], replicated, may hold values from -3 to 3
- inner_bias: float32 [3072], replicated, may hold values from -3 to 3
- outer_bias: float32 [768], replicated, may hold values from -3 to 3
- attn_gain: float32 [768], replicated, may hold values from 0.25 to 1.75
- attn_shift: float32 [768], replicated, may hold values from -3 to 3
- ffn_gain: float32 [768], replicated, may hold values from 0.25 to 1.75
- ffn_shift: float32 [768], replicated, may hold values from -3 to 3
- cotangent: bfloat16 [16384, 768], P(('rep', 'shard')), may hold values from -6 to 6
Outputs:
- layer_output: bfloat16 [16384, 768], P(('rep', 'shard'))
- input_grad: float32 [16384, 768], P(('rep', 'shard'))
- grad_query_weight: float32 [768, 768], P('shard')
- grad_key_weight: float32 [768, 768], P('shard')
- grad_value_weight: float32 [768, 768], P('shard')
- grad_output_weight: float32 [768, 768], P('shard')
- grad_inner_weight: float32 [768, 3072], P('shard')
- grad_outer_weight: float32 [3072, 768], P('shard')
- grad_query_bias: float32 [768], replicated
- grad_value_bias: float32 [768], replicated
- grad_output_bias: float32 [768], replicated
- grad_inner_bias: float32 [3072], replicated
- grad_outer_bias: float32 [768], replicated
- grad_attn_gain: float32 [768], replicated
- grad_attn_shift: float32 [768], replicated
- grad_ffn_gain: float32 [768], replicated
- grad_ffn_shift: float32 [768], replicated
The draws below stay inside these ranges and needn't reach their ends.
All inputs are finite; a program needn't handle non-finite values.
Results may differ from the reference program's by a relative error of at most 0.02.
Values may be sent and summed in bfloat16 or wider, within the bound.
A program may use at most 128 MiB of HBM per device.

```python
import jax
import jax.numpy as jnp
from jax import lax

D = 768
HEADS = 12
FF = 3072
HD = 64
LEN = 512
SEQS = 32
TOKENS = 16384


def block_scale(stream_key, shape, split, least, high):
    level = 1.0
    for dim, parts in split:
        heights = jax.random.uniform(jax.random.fold_in(jax.random.fold_in(stream_key, 6), dim), (parts,), jnp.float32, least / len(split), high / len(split))
        level = level * jnp.repeat(jnp.exp(heights), shape[dim] // parts).reshape((-1,) + (1,) * (len(shape) - 1 - dim))
    return level


def normal_values(own_key, dims, width, bound, pieces=(), kind=jnp.bfloat16):
    gain = block_scale(own_key, dims, pieces, -0.22, 0.18) if pieces else 1.0
    array = jax.random.normal(own_key, dims, jnp.float32) * width * gain
    return jnp.minimum(jnp.maximum(array, -bound), bound).astype(kind)


def setup_inputs(seed: int = 0) -> dict:
    splits = jax.random.split(jax.random.key(seed), 18)
    layer_input = normal_values(splits[0], (TOKENS, D), 1.0, 6.0, ((0, 32),))
    query_weight = normal_values(splits[1], (D, D), D ** -0.5, 0.21875, ((0, 4),))
    key_weight = normal_values(splits[2], (D, D), D ** -0.5, 0.21875, ((0, 4),))
    value_weight = normal_values(splits[3], (D, D), D ** -0.5, 0.21875, ((0, 4),))
    output_weight = normal_values(splits[4], (D, D), (max(D // LEN, 1)) ** -0.5, 6.0, ((0, 4),))
    inner_weight = normal_values(splits[5], (D, FF), D ** -0.5, 0.21875, ((0, 4),))
    outer_weight = normal_values(splits[6], (FF, D), FF ** -0.5, 0.109375, ((0, 4),))
    query_bias = normal_values(splits[7], (D,), 0.5, 3.0, (), jnp.float32)
    value_bias = normal_values(splits[8], (D,), 0.5, 3.0, (), jnp.float32)
    output_bias = normal_values(splits[9], (D,), 0.5, 3.0, (), jnp.float32)
    inner_bias = normal_values(splits[10], (FF,), 0.5, 3.0, (), jnp.float32)
    outer_bias = normal_values(splits[11], (D,), 0.5, 3.0, (), jnp.float32)
    attn_gain = jnp.clip(1.0 + 0.15 * jax.random.normal(splits[12], (D,), jnp.float32), 0.25, 1.75)
    attn_shift = normal_values(splits[13], (D,), 0.5, 3.0, (), jnp.float32)
    ffn_gain = jnp.clip(1.0 + 0.15 * jax.random.normal(splits[14], (D,), jnp.float32), 0.25, 1.75)
    ffn_shift = normal_values(splits[15], (D,), 0.5, 3.0, (), jnp.float32)
    cotangent = normal_values(splits[16], (TOKENS, D), 1.0, 6.0, ((0, 32),))
    return dict(layer_input=layer_input, query_weight=query_weight, key_weight=key_weight, value_weight=value_weight, output_weight=output_weight, inner_weight=inner_weight, outer_weight=outer_weight, query_bias=query_bias, value_bias=value_bias, output_bias=output_bias, inner_bias=inner_bias, outer_bias=outer_bias, attn_gain=attn_gain, attn_shift=attn_shift, ffn_gain=ffn_gain, ffn_shift=ffn_shift, cotangent=cotangent)


@jax.custom_vjp
def low(v):
    return lax.optimization_barrier(v.astype(jnp.bfloat16)).astype(jnp.float32)

@jax.custom_vjp
def low_back(v):
    return v

def low_keep(v):
    return (low(v), None)

def low_pass(kept, grad):
    return (grad,)

def back_keep(v):
    return (v, None)

def back_low(kept, grad):
    return (low(grad),)
low.defvjp(low_keep, low_pass)
low_back.defvjp(back_keep, back_low)
eps_norm = 1e-05

def matmul(left, right):
    return jnp.dot(left, right, precision=lax.Precision.HIGHEST, preferred_element_type=jnp.float32)

def layer_norm(values, norm_gain, norm_shift):
    row_mean = lax.optimization_barrier(jnp.mean(values, axis=-1, keepdims=True))
    centered = values - row_mean
    variance = lax.optimization_barrier(jnp.mean(centered * centered, axis=-1, keepdims=True))
    return centered * lax.rsqrt(variance + eps_norm) * norm_gain + norm_shift

def attention(query_rows, key_rows, value_rows):
    groups, length = (query_rows.shape[0], query_rows.shape[1])
    query_heads = query_rows.reshape(groups, length, HEADS, HD)
    key_heads = key_rows.reshape(groups, length, HEADS, HD)
    value_heads = value_rows.reshape(groups, length, HEADS, HD)
    raw_scores = jnp.einsum('gqhd,gkhd->ghqk', query_heads, key_heads, precision=lax.Precision.HIGHEST)
    scores = low_back(raw_scores) * HD ** (-0.5)
    attn_probs = low(jax.nn.softmax(scores, axis=-1))
    context = jnp.einsum('ghqk,gkhd->gqhd', attn_probs, value_heads, precision=lax.Precision.HIGHEST)
    return context.reshape(groups, length, HEADS * HD)

def layer_block(tokens, params):
    query_weight, key_weight, value_weight, output_weight, inner_weight, outer_weight, query_bias, value_bias, output_bias, inner_bias, outer_bias, attn_gain, attn_shift, ffn_gain, ffn_shift = params
    query_rows = low_back(low(matmul(tokens, query_weight) + query_bias))
    key_rows = low_back(low(matmul(tokens, key_weight)))
    value_rows = low_back(low(matmul(tokens, value_weight) + value_bias))
    context = low_back(low(attention(query_rows, key_rows, value_rows)))
    mixed = low_back(matmul(context, output_weight) + output_bias)
    first_norm = layer_norm(tokens + mixed, attn_gain, attn_shift)
    pre_act = low_back(matmul(low(first_norm), inner_weight) + inner_bias)
    hidden = low(jax.nn.gelu(pre_act, approximate=False))
    outer = low_back(matmul(hidden, outer_weight) + outer_bias)
    return layer_norm(first_norm + outer, ffn_gain, ffn_shift)

def reference(layer_input, query_weight, key_weight, value_weight, output_weight, inner_weight, outer_weight, query_bias, value_bias, output_bias, inner_bias, outer_bias, attn_gain, attn_shift, ffn_gain, ffn_shift, cotangent):
    params = tuple((member.astype(jnp.float32) for member in (query_weight, key_weight, value_weight, output_weight, inner_weight, outer_weight, query_bias, value_bias, output_bias, inner_bias, outer_bias, attn_gain, attn_shift, ffn_gain, ffn_shift)))
    per_step = 1
    while per_step * 2 * LEN <= 4096 and SEQS % (per_step * 2) == 0:
        per_step = per_step * 2
    tokens = layer_input.astype(jnp.float32).reshape(SEQS // per_step, per_step, LEN, D)
    incoming = cotangent.astype(jnp.float32).reshape(SEQS // per_step, per_step, LEN, D)

    def run_all(tokens_all, params_all):
        step_fn = jax.checkpoint(lambda block_in: layer_block(block_in, params_all))
        return lax.map(step_fn, tokens_all)
    output, pullback = jax.vjp(run_all, tokens, params)
    grad_tokens, grad_params = pullback(incoming)
    return (output.reshape(TOKENS, D).astype(jnp.bfloat16), grad_tokens.reshape(TOKENS, D), grad_params[0], grad_params[1], grad_params[2], grad_params[3], grad_params[4], grad_params[5], grad_params[6], grad_params[7], grad_params[8], grad_params[9], grad_params[10], grad_params[11], grad_params[12], grad_params[13], grad_params[14])
```

```python
from functools import partial

import jax
import jax.numpy as jnp
from jax import lax
from jax.experimental import pallas as pl
from jax.experimental.pallas import tpu as pltpu
from jax.sharding import PartitionSpec as P

HEADS = 12
HD = 64
LEN = 512
D = 768
FF = 3072
EPS = 1e-05
ERF_P = 0.43
ERF_C = (0.2425386708813374, 0.24398923753041435, 0.20746461354880297, 0.2382254793532983, -0.06885152354982843, 0.3647704954681695, -0.29905190193018827, 0.0709147474121678)
F32 = jnp.float32
BF16 = jnp.bfloat16
MESH = pl.DeviceIdType.MESH


def nn(a, b):
    return jnp.dot(a, b, preferred_element_type=F32)


def nt(a, b):
    return lax.dot_general(a, b, (((1,), (1,)), ((), ())), preferred_element_type=F32)


def tn(a, b):
    return lax.dot_general(a, b, (((0,), (0,)), ((), ())), preferred_element_type=F32)


def norm_cdf_pdf(v):
    e = jnp.exp(v * v * (-0.5))
    t = 1.0 / (1.0 + (ERF_P * 0.7071067811865476) * jnp.abs(v))
    poly = jnp.full_like(t, ERF_C[-1])
    for coef in ERF_C[-2::-1]:
        poly = poly * t + coef
    half = (0.5 * t) * poly * e
    return jnp.where(v >= 0, 1.0 - half, half), e * 0.3989422804014327


def fold8(v):
    return jnp.sum(v.reshape(v.shape[0] // 8, 8, v.shape[1]), axis=0)


def whole(w):
    return w[...].reshape(w.shape[0] * w.shape[1], w.shape[2])


class Ctx:
    pass


def ph_qkv(s):
    for w, b, dst in ((s.wq, s.bq, s.q), (s.wk, None, s.k), (s.wv, s.bv, s.v)):
        @pl.loop(0, 3)
        def _(j):
            cols = pl.ds(pl.multiple_of(j * 256, 256), 256)
            r = nn(s.x[...], w[:, :, cols].reshape(D, 256))
            if b is not None:
                r = r + b[:, cols]
            if dst is s.q:
                r = r.astype(BF16).astype(F32) * (HD ** -0.5)
            dst[:, cols] = r.astype(BF16)


def ph_transpose(src, dst, n):
    @pl.loop(0, n // 128)
    def _(j):
        c = pl.ds(pl.multiple_of(j * 128, 128), 128)
        dst[c, :] = src[:, c].T


def ph_untranspose(src, dst, n):
    @pl.loop(0, n // 128)
    def _(j):
        c = pl.ds(pl.multiple_of(j * 128, 128), 128)
        dst[:, c] = src[c, :].T


def head_mask(h):
    lane = lax.broadcasted_iota(jnp.int32, (1, 128), 1)
    return (lane < HD) if h == 0 else (lane >= HD)


def ph_attend(s, lo, hi):
    @pl.loop(lo, hi)
    def _(j):
        c = pl.ds(pl.multiple_of(j * 128, 128), 128)
        kp = s.k[:, c]
        qp = s.q[:, c]
        for h in range(2):
            km = jnp.where(head_mask(h), kp, jnp.zeros_like(kp))
            st = nt(km, qp)
            m = jnp.max(st, axis=0, keepdims=True)
            e = jnp.exp(st - m)
            tot = jnp.sum(e, axis=0, keepdims=True)
            p = (e * (1.0 / tot)).astype(BF16)
            s.probs[2 * j + h] = p
            rows = pl.ds(pl.multiple_of(j * 128 + h * HD, HD), HD)
            s.ctxT[rows, :] = nn(s.vT[rows, :], p).astype(BF16)


def ph_first(s):
    @pl.loop(0, 2)
    def _(i):
        r = pl.ds(pl.multiple_of(i * 256, 256), 256)
        s.acc[r, :] = nn(s.ctx[r, :], whole(s.wo))

    @pl.loop(0, 8)
    def _(i):
        r = pl.ds(pl.multiple_of(i * 64, 64), 64)
        v = s.acc[r, :] + s.x[r, :].astype(F32) + s.bo[...]
        mean = jnp.mean(v, axis=-1, keepdims=True)
        cen = v - mean
        var = jnp.mean(cen * cen, axis=-1, keepdims=True)
        rstd = lax.rsqrt(var + EPS)
        n = cen * rstd
        s.n1[r, :] = n.astype(s.n1.dtype)
        s.r1[r, :] = jnp.broadcast_to(rstd, (64, 128))
        first = n * s.g1[...] + s.b1[...]
        s.fl[r, :] = first.astype(BF16)
        s.acc[r, :] = first + s.b2[...]


def ph_ffn_up(s, lo, hi):
    @pl.loop(lo, hi)
    def _(j):
        c = pl.ds(pl.multiple_of(j * 256, 256), 256)
        s.pre[...] = nn(s.fl[...], s.wi[:, :, c].reshape(D, 256))
        bias = s.bi[:, c]

        @pl.loop(0, 8, unroll=True)
        def _(i):
            r = pl.ds(i * 64, 64)
            v = s.pre[r, :] + bias
            cdf, pdf = norm_cdf_pdf(v)
            s.hid[r, c] = (v * cdf).astype(BF16)
            s.dact[r, c] = (cdf + v * pdf).astype(BF16)


def ph_ffn_down(s):
    rows = s.w2.shape[1]

    @pl.loop(0, FF // rows)
    def _(j):
        c = pl.ds(pl.multiple_of(j * rows, rows), rows)
        s.acc[...] += nn(s.hid[:, c], s.w2[j])


def ph_second(s):
    zero = jnp.zeros((8, D), F32)

    def body(i, carry):
        dg, db, dbo = carry
        r = pl.ds(pl.multiple_of(i * 64, 64), 64)
        v = s.acc[r, :]
        mean = jnp.mean(v, axis=-1, keepdims=True)
        cen = v - mean
        var = jnp.mean(cen * cen, axis=-1, keepdims=True)
        rstd = lax.rsqrt(var + EPS)
        n = cen * rstd
        cot = s.cot[r, :].astype(F32)
        s.out[r, :] = (n * s.g2[...] + s.sh2[...]).astype(BF16)
        cn = cot * n
        gc = cot * s.g2[...]
        m1 = jnp.mean(gc, axis=-1, keepdims=True)
        m2 = jnp.mean(gc * n, axis=-1, keepdims=True)
        g = rstd * (gc - m1 - n * m2)
        s.acc[r, :] = g
        low = g.astype(BF16)
        s.go[r, :] = low
        return dg + fold8(cn), db + fold8(cot), dbo + fold8(low.astype(F32))

    dg, db, dbo = lax.fori_loop(0, 8, body, (zero, zero, zero))
    s.small[6:7, :] = jnp.sum(dg, axis=0, keepdims=True)
    s.small[7:8, :] = jnp.sum(db, axis=0, keepdims=True)
    s.small[3:4, :] = jnp.sum(dbo, axis=0, keepdims=True)


def ph_ffn_back_a(s, lo, hi):
    tile = 256 if s.w2.shape[1] % 256 == 0 else 128
    per = s.w2.shape[1] // tile

    @pl.loop(lo * 256 // tile, hi * 256 // tile)
    def _(j):
        c = pl.ds(pl.multiple_of(j * tile, tile), tile)
        z = j // per
        p = j - z * per
        w = pl.ds(pl.multiple_of(p * tile, tile), tile)
        s.pre[:, :tile] = nt(s.go[...], s.w2[z, w, :])
        s.w2[z, w, :] = tn(s.hid[:, c], s.go[...]).astype(BF16)
        tot = jnp.zeros((8, tile), F32)
        for i in range(8):
            r = pl.ds(i * 64, 64)
            g = (s.pre[r, :tile] * s.dact[r, c].astype(F32)).astype(BF16)
            s.hid[r, c] = g
            tot = tot + fold8(g.astype(F32))
        s.ib[0:1, c] = jnp.sum(tot, axis=0, keepdims=True)


def ph_ffn_back_b(s, lo, hi, step):
    shape = s.wi.shape

    @pl.loop(lo, hi, step=step)
    def _(j):
        c = pl.ds(pl.multiple_of(j * D, D), D)
        s.acc[...] += nt(s.hid[:, c], s.wi[:, :, c].reshape(D, D))
        s.wi[:, :, c] = nn(s.flT[...], s.hid[:, c]).astype(BF16).reshape(shape[0], shape[1], D)


def ph_first_back(s):
    zero = jnp.zeros((8, D), F32)

    def body(i, carry):
        dg, db, dbo = carry
        r = pl.ds(pl.multiple_of(i * 64, 64), 64)
        n = s.n1[r, :].astype(F32)
        rstd = s.r1[r, :][:, 0:1]
        gf = s.acc[r, :]
        gc = gf * s.g1[...]
        m1 = jnp.mean(gc, axis=-1, keepdims=True)
        m2 = jnp.mean(gc * n, axis=-1, keepdims=True)
        g = rstd * (gc - m1 - n * m2)
        s.acc[r, :] = g
        low = g.astype(BF16)
        s.gm[r, :] = low
        return dg + fold8(gf * n), db + fold8(gf), dbo + fold8(low.astype(F32))

    dg, db, dbo = lax.fori_loop(0, 8, body, (zero, zero, zero))
    s.small[4:5, :] = jnp.sum(dg, axis=0, keepdims=True)
    s.small[5:6, :] = jnp.sum(db, axis=0, keepdims=True)
    s.small[2:3, :] = jnp.sum(dbo, axis=0, keepdims=True)


def ph_out_back(s):
    @pl.loop(0, 2)
    def _(i):
        r = pl.ds(pl.multiple_of(i * 256, 256), 256)
        s.gc[r, :] = nt(s.gm[r, :], whole(s.wo)).astype(BF16)
    weight_grad(s.ctxT, s.gm, s.wo)


def ph_attend_back(s, lo, hi):
    @pl.loop(lo, hi)
    def _(j):
        c = pl.ds(pl.multiple_of(j * 128, 128), 128)
        vp = s.v[:, c]
        gp = s.gc[:, c]
        qp = s.q[:, c]
        dk = []
        dv = []
        for h in range(2):
            vm = jnp.where(head_mask(h), vp, jnp.zeros_like(vp))
            p = s.probs[2 * j + h]
            dp = nt(vm, gp)
            pf = p.astype(F32)
            pd = pf * dp
            rd = jnp.sum(pd, axis=0, keepdims=True)
            ds = (pd - pf * rd).astype(BF16)
            rows = pl.ds(pl.multiple_of(j * 128 + h * HD, HD), HD)
            s.dqT[rows, :] = (nn(s.kT[rows, :], ds) * (HD ** -0.5)).astype(BF16)
            dk.append(nn(ds, qp))
            dv.append(nn(p, gp))
        s.dk[:, c] = jnp.where(head_mask(0), dk[0], dk[1]).astype(BF16)
        s.dv[:, c] = jnp.where(head_mask(0), dv[0], dv[1]).astype(BF16)
        s.dq[:, c] = s.dqT[c, :].T


def colsum(src, small, row):
    def body(i, tot):
        r = pl.ds(pl.multiple_of(i * 64, 64), 64)
        return tot + fold8(src[r, :].astype(F32))
    tot = lax.fori_loop(0, 8, body, jnp.zeros((8, D), F32))
    small[row:row + 1, :] = jnp.sum(tot, axis=0, keepdims=True)


def weight_grad(leftT, right, w):
    rows = w.shape[1]

    @pl.loop(0, w.shape[0])
    def _(j):
        w[j] = nn(leftT[pl.ds(pl.multiple_of(j * rows, rows), rows), :], right[...]).astype(BF16)


def ph_in_back(s):
    @pl.loop(0, 2)
    def _(i):
        r = pl.ds(pl.multiple_of(i * 256, 256), 256)
        s.ig[r, :] = s.acc[r, :] + nt(s.dq[r, :], whole(s.wq)) + nt(s.dk[r, :], whole(s.wk)) + nt(s.dv[r, :], whole(s.wv))


class Net:
    def __init__(self, send_sem, recv_sem):
        self.send_sem, self.recv_sem, self.count = send_sem, recv_sem, 0
        rep = lax.axis_index("rep")
        self.z = lax.axis_index("shard")
        self.rep, self.c, self.q = rep, lax.rem(rep, 2), lax.div(rep, 2)
        self.sent = []

    def partner(self):
        return (self.q * 2 + (1 - self.c), self.z)

    def plane(self, d):
        return (lax.bitwise_xor(self.q, d) * 2 + self.c, self.z)

    def line(self, d):
        return (self.rep, lax.rem(self.z + d, 4))

    def push(self, src, dst, dev):
        i = self.count
        self.count += 1
        cp = pltpu.make_async_remote_copy(src_ref=src, dst_ref=dst, send_sem=self.send_sem.at[i], recv_sem=self.recv_sem.at[i],
                                          device_id=dev, device_id_type=MESH)
        cp.start()
        self.sent.append(cp)
        return cp

    def drain(self):
        for cp in self.sent:
            cp.wait_send()
        self.sent = []

    def barrier(self):
        bar = pltpu.get_barrier_semaphore()
        peers = [self.partner()] + [self.plane(d) for d in (1, 2, 3)] + [self.line(d) for d in (1, 2, 3)]
        for dev in peers:
            pl.semaphore_signal(bar, inc=1, device_id=dev, device_id_type=MESH)
        pl.semaphore_wait(bar, len(peers))


def arrived(copies):
    for cp in copies:
        cp.wait_recv()


def span(start, size):
    return pl.ds(pl.multiple_of(start, size), size)


class Gather:
    def __init__(self, net, shard, full, relay):
        self.net, self.shard, self.full, self.relay = net, shard, full, relay
        _, self.rz, n = full.shape
        self.rq, self.nh = self.rz // 4, n // 2
        self.cols = span(net.c * self.nh, self.nh)

    def rows(self, q):
        return span(q * self.rq, self.rq)

    def line(self):
        net = self.net
        r = self.rows(net.q)
        self.a = [net.push(self.shard.at[r, self.cols], self.full.at[net.z, r, self.cols], net.line(d)) for d in (1, 2, 3)]

    def plane(self):
        net = self.net
        arrived(self.a)
        r = self.rows(net.q)
        self.b = []
        for d in (1, 2, 3):
            ref = self.full.at[lax.rem(net.z + d, 4), r, self.cols]
            self.b += [net.push(ref, ref, net.plane(1)), net.push(ref, ref, net.plane(2))]

    def diagonal(self):
        net = self.net
        arrived(self.b)
        self.e = []
        for d in (1, 2, 3):
            zz = lax.rem(net.z + d, 4)
            for via in (1, 2):
                q = lax.bitwise_xor(net.q, 3 - via)
                if self.relay == "rows":
                    h = self.rq // 2
                    ref = self.full.at[zz, span(q * self.rq + (via - 1) * h, h), self.cols]
                elif self.relay == "cols":
                    h = self.nh // 2
                    ref = self.full.at[zz, self.rows(q), span(net.c * self.nh + (via - 1) * h, h)]
                elif self.relay == via:
                    ref = self.full.at[zz, self.rows(q), self.cols]
                else:
                    continue
                self.e.append(net.push(ref, ref, net.plane(via)))

    def share(self):
        net = self.net
        arrived(self.e)
        self.f = []
        for d in (1, 2, 3):
            ref = self.full.at[lax.rem(net.z + d, 4), :, self.cols]
            self.f.append(net.push(ref, ref, net.partner()))

    def done(self):
        arrived(self.f)


class Reduce:
    def __init__(self, net, full, first, part, got, bufs):
        self.net, self.full, self.first, self.second = net, full, first, 3 - first
        _, self.rz, n = full.shape
        self.rq, nh = self.rz // 4, n // 2
        self.nh = nh
        self.pb, self.ab, self.bb, self.zb = bufs
        self.got = got
        kind, k = part
        self.ro, self.rn, self.co, self.cn = 0, self.rq, 0, nh
        if kind == "rows":
            self.rn = self.rq // 2
            self.ro = k * self.rn
        elif kind == "cols":
            self.cn = nh // 2
            self.co = k * self.cn
        self.cols = span(net.c * nh + self.co, self.cn)

    def rows(self, q):
        return span(q * self.rq + self.ro, self.rn)

    def a_send(self):
        net = self.net
        near = lax.bitwise_xor(net.q, self.first)
        far = lax.bitwise_xor(net.q, 3)
        self.a = [net.push(self.full.at[:, self.rows(near), self.cols], self.ab.at[0], net.plane(self.first)),
                  net.push(self.full.at[:, self.rows(far), self.cols], self.ab.at[1], net.plane(self.first))]

    def add(self, q, zs, srcs):
        step = 16

        def body(j, _):
            k = j // (self.rn // step)
            o = (j - k * (self.rn // step)) * step
            r = pl.ds(pl.multiple_of(q * self.rq + self.ro + o, step), step)
            o = pl.ds(pl.multiple_of(o, step), step)
            z = zs if zs is not None else k
            v = self.full[z, r, self.cols].astype(F32)
            for src in srcs:
                v = v + src(k, o).astype(F32)
            self.full[z, r, self.cols] = v.astype(BF16)
            return 0

        lax.fori_loop(0, (1 if zs is not None else 4) * (self.rn // step), body, 0)

    def b_send(self):
        net = self.net
        arrived(self.a)
        mid = lax.bitwise_xor(net.q, self.second)
        self.add(mid, None, [lambda k, o: self.ab[1, k, o, :]])
        self.b = net.push(self.full.at[:, self.rows(mid), self.cols], self.bb, net.plane(self.second))
        self.add(net.q, None, [lambda k, o: self.ab[0, k, o, :]])

    def z_send(self):
        net = self.net
        arrived([self.b])
        self.add(net.q, None, [lambda k, o: self.bb[k, o, :]])
        self.zc = [net.push(self.full.at[lax.rem(net.z + d, 4), self.rows(net.q), self.cols], self.zb.at[d - 1], net.line(d)) for d in (1, 2, 3)]

    def f_send(self, sem):
        net = self.net
        arrived(self.zc)
        self.add(net.q, net.z, [lambda k, o, d=d: self.zb[d, o, :] for d in range(3)])
        src = self.full.at[net.z, self.rows(net.q), self.cols]
        dst = self.got.at[self.rows(net.q), self.cols]
        self.own = pltpu.make_async_copy(src, dst, sem)
        self.own.start()
        self.f = [net.push(src, dst, net.plane(d)) for d in (1, 2, 3)]


class Halves:
    def __init__(self, net, full, pb, part):
        self.net, self.full, self.pb = net, full, pb
        _, self.rz, n = full.shape
        self.nh = n // 2
        self.co, self.cn = 0, self.nh
        if part[0] == "cols":
            self.cn = self.nh // 2
            self.co = part[1] * self.cn

    def send(self):
        net = self.net
        ref = self.full.at[:, :, span((1 - net.c) * self.nh + self.co, self.cn)]
        self.p = net.push(ref, self.pb, net.partner())

    def take(self):
        net = self.net
        arrived([self.p])
        cols = span(net.c * self.nh + self.co, self.cn)
        step = 16
        per = self.rz // step

        def body(j, _):
            k = j // per
            r = pl.ds(pl.multiple_of((j - k * per) * step, step), step)
            self.full[k, r, cols] = (self.full[k, r, cols].astype(F32) + self.pb[k, r, :].astype(F32)).astype(BF16)
            return 0

        lax.fori_loop(0, 4 * per, body, 0)


def back_rows(net, reds):
    for u in reds:
        u.own.wait()
        arrived(u.f)
    got = reds[0].got
    nh = reds[0].nh
    ref = got.at[:, span(net.c * nh, nh)]
    return net.push(ref, ref, net.partner())


def recv_list(shards):
    vm = pltpu.VMEM
    out = {}
    for name, rz, n, parts in (("q", shards[0], D, 1), ("k", shards[0], D, 1), ("v", shards[0], D, 1), ("o", shards[0], D, 1),
                               ("i", shards[0], FF, 2), ("2", shards[1], D, 2)):
        rows = rz if name == "2" else rz
        for u in range(parts):
            cn = n // 2 // (parts if name == "i" else 1)
            rn = rz // 4 // (parts if name == "2" else 1)
            if not (name == "2" and u == 1):
                out["pb%s%d" % (name, u)] = vm((4, rows, cn), BF16)
            out["ab%s%d" % (name, u)] = vm((2, 4, rn, cn), BF16)
            out["bb%s%d" % (name, u)] = vm((4, rn, cn), BF16)
            out["zb%s%d" % (name, u)] = vm((3, rn, cn), BF16)
    out["sp"] = vm((16, D), F32)
    out["sq"] = vm((4, 16, D), F32)
    out["sz"] = vm((4, 16, D), F32)
    out["send"] = pltpu.SemaphoreType.DMA((COPIES,))
    out["recv"] = pltpu.SemaphoreType.DMA((COPIES,))
    return out


COPIES = 256


def scratch_list(shards, comm):
    vm = pltpu.VMEM
    r1, r2 = shards
    n = D // r1
    out = dict(
        wq=vm((n, r1, D), BF16), wk=vm((n, r1, D), BF16), wv=vm((n, r1, D), BF16), wo=vm((n, r1, D), BF16),
        wi=vm((n, r1, FF), BF16), w2=vm((n, r2, D), BF16),
        x=vm((LEN, D), BF16), cot=vm((LEN, D), BF16), xT=vm((D, LEN), BF16),
        q=vm((LEN, D), BF16), k=vm((LEN, D), BF16), v=vm((LEN, D), BF16),
        kT=vm((D, LEN), BF16), vT=vm((D, LEN), BF16),
        probs=vm((HEADS, LEN, LEN), BF16), ctxT=vm((D, LEN), BF16), ctx=vm((LEN, D), BF16),
        acc=vm((LEN, D), F32), n1=vm((LEN, D), F32), r1=vm((LEN, 128), F32),
        fl=vm((LEN, D), BF16), flT=vm((D, LEN), BF16),
        pre=vm((LEN, 256), F32), hid=vm((LEN, FF), BF16), dact=vm((LEN, FF), BF16),
        go=vm((LEN, D), BF16), small=vm((16, D), F32), ib=vm((8, FF), F32),
        sem=pltpu.SemaphoreType.DMA((24,)),
    )
    if comm:
        out.update(recv_list(shards))
    return out


def layer_kernel(names, comm, x_h, wq_h, wk_h, wv_h, wo_h, wi_h, w2_h, bq, bv, bo, bi, b2, g1, b1, g2, sh2, cot_h,
                 out_h, ig_h, dq_h, dk_h, dv_h, do_h, di_h, d2_h, small_out, *scratch):
    s = Ctx()
    for n, r in zip(names, scratch):
        setattr(s, n, r)
    s.bq, s.bv, s.bo, s.bi, s.b2, s.g1, s.b1, s.g2, s.sh2 = bq, bv, bo, bi, b2, g1, b1, g2, sh2
    s.out = s.cot
    s.gm = s.go
    s.gc = s.ctx
    s.dqT = s.vT
    s.dq, s.dk, s.dv = s.q, s.k, s.v
    s.ig = s.acc
    weights = (s.wq, s.wk, s.wv, s.wo, s.wi, s.w2)
    shards = (wq_h, wk_h, wv_h, wo_h, wi_h, w2_h)
    grads = (dq_h, dk_h, dv_h, do_h, di_h, d2_h)
    if comm:
        net = Net(s.send, s.recv)
        net.barrier()
        gq, gk, gv, go, gi, g2w = gs = [Gather(net, a, b, r) for a, b, r in zip(shards, weights, (1, 2, 1, 2, "cols", "rows"))]
        for g in gs:
            g.line()
        dst = [w.at[net.z] for w in weights]
    else:
        dst = list(weights)
    cps = [pltpu.make_async_copy(a, b, s.sem.at[i]) for i, (a, b) in
           enumerate(zip((x_h, *shards, cot_h), (s.x, *dst, s.cot)))]
    for c in cps:
        c.start()
    s.small[...] = jnp.zeros_like(s.small)
    cps[0].wait()
    ph_transpose(s.x, s.xT, D)
    if comm:
        for g in (gq, gk, gv, go):
            g.plane()
        for g in (gq, gk, gv, go):
            g.diagonal()
        for g in (gq, gk, gv):
            g.share()
        for g in (gq, gk, gv):
            g.done()
    for i in (1, 2, 3):
        cps[i].wait()
    ph_qkv(s)
    ph_transpose(s.k, s.kT, D)
    ph_transpose(s.v, s.vT, D)
    if comm:
        gi.plane()
        go.share()
        ph_attend(s, 0, 2)
        gi.diagonal()
        ph_attend(s, 2, 4)
        g2w.plane()
        ph_attend(s, 4, 6)
        gi.share()
        go.done()
    else:
        ph_attend(s, 0, 6)
    ph_untranspose(s.ctxT, s.ctx, D)
    cps[4].wait()
    ph_first(s)
    ph_transpose(s.fl, s.flT, D)
    cps[5].wait()
    cps[6].wait()
    if comm:
        gi.done()
        ph_ffn_up(s, 0, 6)
        g2w.diagonal()
        ph_ffn_up(s, 6, 12)
        g2w.share()
        g2w.done()
        net.drain()
    else:
        ph_ffn_up(s, 0, 12)
    ph_ffn_down(s)
    cps[7].wait()
    ph_second(s)
    ocp = pltpu.make_async_copy(s.out, out_h, s.sem.at[0])
    ocp.start()
    ph_ffn_back_a(s, 0, 12)
    for i in range(4):
        s.small[8 + i:9 + i, :] = s.ib[0:1, i * D:(i + 1) * D]
    if not comm:
        ph_ffn_back_b(s, 0, 4, 1)
        ph_first_back(s)
        ph_out_back(s)
        ph_attend_back(s, 0, 6)
        ph_in_back(s)
        icp = pltpu.make_async_copy(s.ig, ig_h, s.sem.at[1])
        icp.start()
        weight_grad(s.xT, s.dq, s.wq)
        weight_grad(s.xT, s.dk, s.wk)
        weight_grad(s.xT, s.dv, s.wv)
        colsum(s.dq, s.small, 0)
        colsum(s.dv, s.small, 1)
        cps = [pltpu.make_async_copy(a, b, s.sem.at[i + 2]) for i, (a, b) in enumerate(zip(weights, grads))]
        for c in cps:
            c.start()
        small_out[...] = s.small[...]
        for c in (ocp, icp, *cps):
            c.wait()
        return

    def unit(w, first, part, got, name):
        return Reduce(net, w, first, part, got, [getattr(s, b + name, None) for b in ("pb", "ab", "bb", "zb")])

    one = ("all", 0)
    u20, u21 = unit(s.w2, 1, ("rows", 0), d2_h, "20"), unit(s.w2, 2, ("rows", 1), d2_h, "21")
    ui0, ui1 = unit(s.wi, 1, ("cols", 0), di_h, "i0"), unit(s.wi, 2, ("cols", 1), di_h, "i1")
    uo, uq, uk, uv = (unit(s.wo, 1, one, do_h, "o0"), unit(s.wq, 2, one, dq_h, "q0"),
                      unit(s.wk, 1, one, dk_h, "k0"), unit(s.wv, 2, one, dv_h, "v0"))
    h2, hi0, hi1 = Halves(net, s.w2, s.pb20, one), Halves(net, s.wi, s.pbi0, ("cols", 0)), Halves(net, s.wi, s.pbi1, ("cols", 1))
    ho, hq, hk, hv = (Halves(net, s.wo, s.pbo0, one), Halves(net, s.wq, s.pbq0, one), Halves(net, s.wk, s.pbk0, one),
                      Halves(net, s.wv, s.pbv0, one))
    h2.send()
    ph_ffn_back_b(s, 0, 4, 2)
    hi0.send()
    h2.take()
    u20.a_send()
    u21.a_send()
    ph_ffn_back_b(s, 1, 4, 2)
    hi1.send()
    hi0.take()
    ui0.a_send()
    ph_first_back(s)
    hi1.take()
    ui1.a_send()
    ph_out_back(s)
    ho.send()
    u20.b_send()
    u21.b_send()
    ph_attend_back(s, 0, 2)
    ho.take()
    uo.a_send()
    ui0.b_send()
    ph_attend_back(s, 2, 4)
    ui1.b_send()
    u20.z_send()
    u21.z_send()
    ph_attend_back(s, 4, 6)
    uo.b_send()
    weights_grad = ((s.dq, s.wq, hq), (s.dk, s.wk, hk), (s.dv, s.wv, hv))
    ph_in_back(s)
    icp = pltpu.make_async_copy(s.ig, ig_h, s.sem.at[1])
    icp.start()
    for d, w, h in weights_grad:
        weight_grad(s.xT, d, w)
        h.send()
    colsum(s.dq, s.small, 0)
    colsum(s.dv, s.small, 1)
    sp = net.push(s.small, s.sp, net.partner())
    for h, u in ((hq, uq), (hk, uk), (hv, uv)):
        h.take()
        u.a_send()
    ui0.z_send()
    ui1.z_send()
    arrived([sp])
    s.sq[net.q] = s.small[...] + s.sp[...]
    sq = [net.push(s.sq.at[net.q], s.sq.at[net.q], net.plane(d)) for d in (1, 2, 3)]
    u20.f_send(s.sem.at[8])
    u21.f_send(s.sem.at[9])
    uo.z_send()
    for u in (uq, uk, uv):
        u.b_send()
    arrived(sq)
    s.sz[net.z] = s.sq[0] + s.sq[1] + s.sq[2] + s.sq[3]
    sz = [net.push(s.sz.at[net.z], s.sz.at[net.z], net.line(d)) for d in (1, 2, 3)]
    ui0.f_send(s.sem.at[10])
    ui1.f_send(s.sem.at[11])
    for u in (uq, uk, uv):
        u.z_send()
    uo.f_send(s.sem.at[12])
    last = [back_rows(net, (u20, u21)), back_rows(net, (ui0, ui1))]
    for i, u in enumerate((uq, uk, uv)):
        u.f_send(s.sem.at[13 + i])
    arrived(sz)
    small_out[...] = s.sz[0] + s.sz[1] + s.sz[2] + s.sz[3]
    last.append(back_rows(net, (uo,)))
    for u in (uq, uk, uv):
        last.append(back_rows(net, (u,)))
    arrived(last)
    net.drain()
    ocp.wait()
    icp.wait()


def layer_call(args, comm):
    x, wq, wk, wv, wo, wi, w2, bq, bv, bo, bi, b2, g1, b1, g2, sh2, cot = args
    rows = [v.reshape(1, -1) for v in (bq, bv, bo, bi, b2, g1, b1, g2, sh2)]
    any_ = pl.BlockSpec(memory_space=pl.ANY)
    vmem = pl.BlockSpec(memory_space=pltpu.VMEM)
    sds = jax.ShapeDtypeStruct
    mats = (wq, wk, wv, wo, wi, w2)
    r1, r2 = wq.shape[-2], w2.shape[-2]
    sc = scratch_list((r1, r2), comm)
    params = dict(collective_id=0, has_side_effects=True) if comm else {}
    return pl.pallas_call(
        partial(layer_kernel, tuple(sc), comm),
        out_shape=(sds((LEN, D), BF16), sds((LEN, D), F32), *(sds(w.shape, BF16) for w in mats), sds((16, D), F32)),
        in_specs=[any_] * 7 + [vmem] * 9 + [any_],
        out_specs=(any_,) * 8 + (vmem,),
        scratch_shapes=list(sc.values()),
        compiler_params=pltpu.CompilerParams(vmem_limit_bytes=67043328, **params),
        cost_estimate=pl.CostEstimate(flops=25 * 10 ** 9, bytes_accessed=40 * 10 ** 6, transcendentals=8 * 10 ** 6),
        name="layer",
    )(x, *mats, *rows, cot)


def shards(rep, line, *args):
    x, mats, vecs, cot = args[0], args[1:7], args[7:16], args[16]
    if (rep, line) == (8, 4):
        res = layer_call((x, *mats, *vecs, cot), True)
        grads = [g.astype(F32) for g in res[2:8]]
        small = res[8]
    else:
        full = [lax.all_gather(w, "shard", axis=0) for w in mats]
        res = layer_call((x, *full, *vecs, cot), False)
        grads = [lax.psum(lax.psum_scatter(g, "shard", scatter_dimension=0), "rep").astype(F32) for g in res[2:8]]
        small = lax.psum(res[8], ("rep", "shard"))
    vec = [small[0], small[1], small[2], small[8:12].reshape(FF), small[3], small[4], small[5], small[6], small[7]]
    return (res[0], res[1], *grads, *vec)


def solution(mesh):
    tok = P(("rep", "shard"), None)
    row = P("shard", None)
    return jax.shard_map(
        partial(shards, mesh.shape["rep"], mesh.shape["shard"]),
        mesh=mesh,
        in_specs=(tok,) + (row,) * 6 + (P(),) * 9 + (tok,),
        out_specs=(tok, tok) + (row,) * 6 + (P(),) * 9,
        check_vma=False,
    )
```
